256 devices in a mesh: gx: 16 (over x_hi, z), gy: 8 (over y, core), gz: 2 (over x_lo).
Axes of the slice: x: 4 (x_hi: 2, x_lo: 2; x = x_hi * 2 + x_lo), y: 4, z: 8, core: 2. Of those that a mesh axis runs over, the one named last changes fastest.
Arguments:
- features: bfloat16 [512, 128, 256], P(('gx', 'gy', 'gz')), may hold values from -0.59765625 to 0.59765625
- cotangent: bfloat16 [512, 128, 256], P(('gx', 'gy', 'gz')), may hold values from -6 to 6
- positions: bfloat16 [512, 3, 128], P(('gx', 'gy', 'gz')), may hold values from 0 to 4
- element_types: int32 [512, 128], P(('gx', 'gy', 'gz')), may hold values from 0 to 7
- charge_table: float32 [8], replicated, may hold values from -1.5 to 1.5
- partners: int32 [512, 24], P(('gx', 'gy', 'gz')), may hold values from 0 to 511, as said below
- tile_real_flags: int32 [512, 24], P(('gx', 'gy', 'gz')), may hold values from 0 to 1, as said below
Outputs:
- grad_features: float32 [512, 128, 256], P(('gx', 'gy', 'gz'))
- grad_positions: float32 [512, 3, 128], P(('gx', 'gy', 'gz'))
The draws below stay inside these ranges and needn't reach their ends.
Inputs may be any that keep to these rules, and one draw needn't show every extreme that they name: `partners`: clusters are numbered by device, 2 a device, device number (gx index * size of gy + gy index) * size of gz + gz index; a cluster's local index is 0 or 1. Every entry, padding included, names the other cluster of the same device, or the cluster with local index 0 on the device whose lateral index gx index * size of gy + gy index is one higher (cyclically) and whose gz index is the same, or either cluster of the device one step higher along gz. The live tiles of one cluster name distinct clusters. `tile_real_flags`: A cluster has at most min(24, 4) live tiles, and some cluster has exactly that many.
All inputs are finite; a program needn't handle non-finite values.
Results may differ from the reference program's by a relative error of at most 0.0066.
Values may be sent and summed in bfloat16 or wider, within the bound.
A program may use at most 64 MiB of HBM per device.

```python
import math
import jax
import jax.numpy as jnp
from jax import lax

ATOMS = 128
C = 256
P_SIZE = 24
NE = 8
CLUSTERS_PER_UNIT = 2
LZ = 1
CLUSTERS = 512
N_GZ = 2
DEVICES = 256


def tile_lists(key):
    base_key = jax.random.fold_in(key, 4049)
    draw_keys = jax.random.split(base_key, 4)
    cluster = jnp.arange(CLUSTERS, dtype=jnp.int32)
    device = cluster // CLUSTERS_PER_UNIT
    local_index = cluster % CLUSTERS_PER_UNIT
    lateral = device // N_GZ
    height = device % N_GZ
    lane_count = DEVICES // N_GZ
    own_count = CLUSTERS_PER_UNIT - 1
    cand_total = own_count + LZ + 2
    top_layer = (height == N_GZ - 1).astype(jnp.int32)
    available = cand_total - 2 * top_layer
    cand_index = jnp.arange(cand_total, dtype=jnp.int32)[None, :]
    side_device = (lateral[:, None] + 1) % lane_count * N_GZ + height[:, None]
    upper_device = device[:, None] + 1
    own_pick = device[:, None] * CLUSTERS_PER_UNIT + (local_index[:, None] + 1 + cand_index) % CLUSTERS_PER_UNIT
    side_pick = side_device * CLUSTERS_PER_UNIT + jnp.clip(cand_index - own_count, 0, LZ - 1)
    upper_pick = upper_device * CLUSTERS_PER_UNIT + LZ * jnp.clip(cand_index - own_count - LZ, 0, 1)
    candidate = jnp.where(cand_index < own_count, own_pick, jnp.where(cand_index < own_count + LZ, side_pick, upper_pick))
    valid = cand_index < available[:, None]
    cand_scores = jax.random.randint(draw_keys[0], (CLUSTERS, cand_total), 0, 1048576) * cand_total + cand_index
    cand_scores = jnp.where(valid, cand_scores, cand_scores + 1073741824)
    cand_order = jnp.argsort(cand_scores, axis=1)
    shuffled = jnp.take_along_axis(candidate, cand_order, axis=1)
    grid_shape = (CLUSTERS, P_SIZE)
    slot_scores = jax.random.randint(draw_keys[1], grid_shape, 0, 1048576) * P_SIZE + jnp.arange(P_SIZE, dtype=jnp.int32)
    ranking = jnp.argsort(jnp.argsort(slot_scores, axis=1), axis=1).astype(jnp.int32)
    pick_index = ranking % available[:, None]
    partner = jnp.take_along_axis(shuffled, pick_index, axis=1)
    crowded = jax.random.randint(draw_keys[2], (CLUSTERS,), P_SIZE - P_SIZE // 4, P_SIZE + 1)
    sparse = jax.random.randint(draw_keys[3], (CLUSTERS,), P_SIZE // 4, 3 * P_SIZE // 4 + 1)
    live_count = jnp.where(height == 0, crowded, sparse)
    live_count = jnp.where(cluster == 0, P_SIZE, live_count)
    live_count = jnp.minimum(live_count, available)
    live = (ranking < live_count[:, None]).astype(jnp.int32)
    return (partner.astype(jnp.int32), live)


def draw_partners(key, part):
    return tile_lists(key)[0]


def draw_tile_real_flags(key, part):
    return tile_lists(key)[1]


def set_ends(result, stream_key, least, top_value):
    index_at = [jax.random.randint(jax.random.fold_in(stream_key, axis), (), 0, length) for axis, length in enumerate(result.shape)]
    widest = result.shape.index(max(result.shape))
    beside = index_at[:widest] + [(index_at[widest] + 1) % result.shape[widest]] + index_at[widest + 1:]
    return result.at[tuple(index_at)].set(least).at[tuple(beside)].set(top_value)


def shard_levels(stream_key, extent, pieces, smallest, largest):
    loudness, own = 1.0, jax.random.fold_in(stream_key, 6)
    for dim, shards_of in pieces:
        steps = jnp.exp(jax.random.uniform(jax.random.fold_in(own, dim), (shards_of,), jnp.float32, smallest / len(pieces), largest / len(pieces)))
        loudness = loudness * jnp.repeat(steps, extent[dim] // shards_of).reshape([-1 if axis == dim else 1 for axis in range(len(extent))])
    return loudness


def normal_values(stream_key, extent, deviation, reach, cuts=(), kind=jnp.bfloat16):
    gain = shard_levels(stream_key, extent, cuts, -0.22, 0.18) if cuts else 1.0
    values = jax.random.normal(stream_key, extent, jnp.float32) * deviation * gain
    return jnp.minimum(jnp.maximum(values, -reach), reach).astype(kind)


def setup_inputs(seed: int = 0) -> dict:
    streams_of = jax.random.split(jax.random.key(seed), 8)
    return {
        "features": normal_values(streams_of[0], (CLUSTERS, ATOMS, C), 0.1, 0.59765625, ((0, 256),)),
        "cotangent": normal_values(streams_of[1], (CLUSTERS, ATOMS, C), 1.0, 6.0, ((0, 256),)),
        "positions": jnp.clip(4.0 * jax.random.uniform(streams_of[2], (CLUSTERS, 3, ATOMS), jnp.float32) ** shard_levels(streams_of[2], (CLUSTERS, 3, ATOMS), ((0, 256),), -0.2, 0.2), 0.0, 4.0).astype(jnp.bfloat16),
        "element_types": set_ends(jax.random.randint(streams_of[3], (CLUSTERS, ATOMS), 0, NE), jax.random.fold_in(streams_of[3], 1), 0, NE - 1).astype(jnp.int32),
        "charge_table": jnp.clip(jax.random.uniform(streams_of[4], (NE,), jnp.float32, -1.5, 1.5), -1.5, 1.5),
        "partners": draw_partners(jax.random.fold_in(streams_of[7], 71), 0),
        "tile_real_flags": draw_tile_real_flags(jax.random.fold_in(streams_of[7], 71), 0),
    }


coupling_strength = 0.0625
screening = 0.3
soften = 1.0

def pairwise_terms(nearby_features, nearby_cotangent, remote_features, remote_cotangent, nearby_position_charge, remote_position_charge, tile_real_mask):
    offsets = nearby_position_charge[:, :3, :, None] - remote_position_charge[:, :3, None, :]
    radius = jnp.sqrt(lax.optimization_barrier(jnp.sum(offsets * offsets, axis=1)) + soften)
    atom_charges = nearby_position_charge[:, 3, :, None] * remote_position_charge[:, 3, None, :]
    screen = lax.erfc(screening * radius)
    scaled_terms = coupling_strength * tile_real_mask[:, None, None] * atom_charges
    kernel = lax.optimization_barrier((scaled_terms * screen / radius).astype(jnp.bfloat16)).astype(jnp.float32)
    grad_near = jnp.einsum('txy,tyc->txc', kernel, remote_cotangent)
    grad_far = jnp.einsum('txy,txc->tyc', kernel, nearby_cotangent)
    pair_sum = jnp.einsum('txc,tyc->txy', nearby_cotangent, remote_features) + jnp.einsum('txc,tyc->txy', nearby_features, remote_cotangent)
    slope_term = (-(2.0 * screening / math.sqrt(math.pi)) * jnp.exp(-screening * screening * radius * radius) / radius - screen / (radius * radius)) / radius
    weight = scaled_terms * slope_term * pair_sum
    moved = weight[:, None, :, :] * offsets
    return (grad_near, grad_far, lax.optimization_barrier(jnp.sum(moved, axis=3)), -lax.optimization_barrier(jnp.sum(moved, axis=2)))

def reference(features, cotangent, positions, element_types, charge_table, partners, tile_real_flags):
    charge = charge_table[element_types].astype(jnp.bfloat16)
    position_charge = jnp.concatenate([positions.astype(jnp.float32), charge.astype(jnp.float32)[:, None, :]], axis=1)
    cluster_totals = partners.shape[1]
    blocks = features.shape[0] // CLUSTERS_PER_UNIT
    lane_count = DEVICES // N_GZ

    def tile_step(block_index, totals):
        grad_feat, grad_pos = totals
        block_index = block_index.astype(jnp.int32)
        leading_row = (block_index * CLUSTERS_PER_UNIT).astype(jnp.int32)
        nearby_cluster_rows = leading_row + jnp.repeat(jnp.arange(CLUSTERS_PER_UNIT, dtype=jnp.int32), cluster_totals)
        remote_cluster_rows = lax.dynamic_slice(partners, (leading_row, jnp.int32(0)), (CLUSTERS_PER_UNIT, cluster_totals)).reshape(-1).astype(jnp.int32)
        tile_real_mask = lax.dynamic_slice(tile_real_flags, (leading_row, jnp.int32(0)), (CLUSTERS_PER_UNIT, cluster_totals)).reshape(-1).astype(jnp.float32)
        pairwise_gradient = pairwise_terms(features[nearby_cluster_rows].astype(jnp.float32), cotangent[nearby_cluster_rows].astype(jnp.float32), features[remote_cluster_rows].astype(jnp.float32), cotangent[remote_cluster_rows].astype(jnp.float32), position_charge[nearby_cluster_rows], position_charge[remote_cluster_rows], tile_real_mask)
        own_lateral = block_index // N_GZ
        own_height = block_index % N_GZ
        far_device = remote_cluster_rows // CLUSTERS_PER_UNIT
        is_side = far_device // N_GZ != own_lateral
        is_upper = jnp.logical_and(jnp.logical_not(is_side), far_device % N_GZ != own_height)
        remote = jnp.logical_or(is_side, is_upper)
        slot = jnp.where(is_side, remote_cluster_rows % CLUSTERS_PER_UNIT, jnp.where(is_upper, CLUSTERS_PER_UNIT + remote_cluster_rows % CLUSTERS_PER_UNIT, 2 * CLUSTERS_PER_UNIT)).astype(jnp.int32)
        local_feat = jnp.where(remote[:, None, None], 0.0, pairwise_gradient[1])
        local_pos = jnp.where(remote[:, None, None], 0.0, pairwise_gradient[3])
        grad_feat = grad_feat.at[nearby_cluster_rows].add(pairwise_gradient[0]).at[remote_cluster_rows].add(local_feat)
        grad_pos = grad_pos.at[nearby_cluster_rows].add(pairwise_gradient[2]).at[remote_cluster_rows].add(local_pos)
        feat_buffer = jnp.zeros((2 * CLUSTERS_PER_UNIT + 1,) + features.shape[1:], jnp.float32).at[slot].add(pairwise_gradient[1])
        pos_buffer = jnp.zeros((2 * CLUSTERS_PER_UNIT + 1,) + positions.shape[1:], jnp.float32).at[slot].add(pairwise_gradient[3])
        feat_round = lax.optimization_barrier(feat_buffer[:2 * CLUSTERS_PER_UNIT].astype(jnp.bfloat16)).astype(jnp.float32)
        pos_round = lax.optimization_barrier(pos_buffer[:2 * CLUSTERS_PER_UNIT].astype(jnp.bfloat16)).astype(jnp.float32)
        side_device = (own_lateral + 1) % lane_count * N_GZ + own_height
        upper_device = jnp.minimum(block_index + 1, DEVICES - 1)
        local_ids = jnp.arange(CLUSTERS_PER_UNIT, dtype=jnp.int32)
        targets = jnp.concatenate([side_device * CLUSTERS_PER_UNIT + local_ids, upper_device * CLUSTERS_PER_UNIT + local_ids]).astype(jnp.int32)
        grad_feat = grad_feat.at[targets].add(feat_round)
        grad_pos = grad_pos.at[targets].add(pos_round)
        return (grad_feat, grad_pos)
    start_feat = jnp.zeros(features.shape, jnp.float32)
    start_pos = jnp.zeros(positions.shape, jnp.float32)
    grad_feat, grad_pos = lax.fori_loop(jnp.int32(0), jnp.int32(blocks), tile_step, (start_feat, start_pos))
    return (grad_feat, grad_pos)
```

```python
import math

import jax
import jax.numpy as jnp
from jax import lax
from jax.experimental import pallas as pl
from jax.experimental.pallas import tpu as pltpu
from jax.sharding import PartitionSpec as P

coupling_strength = 0.0625
screening = 0.3
soften = 1.0

AXES = ("gx", "gy", "gz")
MESH = pl.DeviceIdType.MESH
F32, BF16 = jnp.float32, jnp.bfloat16
ROWS = 32

SHIFT = 2.5
SCALED_ERFC = (
    1.0540318489074707, 0.8046519160270691, 0.4539143443107605, 0.171249657869339,
    0.028358077630400658, -0.008383735083043575, -0.004801364149898291, 0.0004147369763813913,
    0.0006639317725785077, -2.737039358180482e-05, -7.203718996606767e-05,
)

OWN, NEXT, PREV, PAIR = "own", "next", "prev", "pair"
TILES = (
    (0, PAIR, 0), (0, PAIR, 1), (0, NEXT, 0), (0, PREV, 0), (0, PREV, 1), (0, OWN, 1),
    (1, PAIR, 0), (1, PAIR, 1), (1, NEXT, 0),
)
SLOT = {tile: n for n, tile in enumerate(TILES)}


def scaled_erfc(x):
    u = 1.0 / (x + SHIFT)
    v = (2.0 * SHIFT) * u - 1.0
    total = jnp.full_like(v, SCALED_ERFC[-1])
    for coefficient in SCALED_ERFC[-2::-1]:
        total = total * v + coefficient
    return total * u


def nt(a, b):
    return lax.dot_general(a, b, (((1,), (1,)), ((), ())), preferred_element_type=F32)


def nn(a, b):
    return lax.dot_general(a, b, (((1,), (0,)), ((), ())), preferred_element_type=F32)


def tn(a, b):
    return lax.dot_general(a, b, (((0,), (0,)), ((), ())), preferred_element_type=F32)


def body(
    gx_size, gy_size,
    feat_hbm, cot_hbm, pos_hbm, elem_hbm, table_ref, part_hbm, flag_hbm,
    out_feat, out_pos,
    feat, cot, pos, elem, part, flag,
    n_feat, n_cot, n_pos, n_elem,
    p_feat, p_cot, p_pos, p_elem, p_part, p_flag,
    z_cot, z_pos, z_elem, z_part, z_flag,
    z_give, z_take,
    wide, kernels, slopes,
    local_sems, send_sems, recv_sems,
):
    gx, gy, gz = lax.axis_index("gx"), lax.axis_index("gy"), lax.axis_index("gz")
    lanes = gx_size * gy_size
    lateral = gx * gy_size + gy
    after = lax.rem(lateral + 1, lanes)
    before = lax.rem(lateral + lanes - 1, lanes)
    next_id = (after // gy_size, lax.rem(after, gy_size), gz)
    prev_id = (before // gy_size, lax.rem(before, gy_size), gz)
    pair_id = (gx, gy, 1 - gz)
    device = lateral * 2 + gz

    barrier = pltpu.get_barrier_semaphore()
    for target in (next_id, prev_id, pair_id):
        pl.semaphore_signal(barrier, inc=1, device_id=target, device_id_type=MESH)

    local = []
    for n, (source, held) in enumerate(
        ((pos_hbm, pos), (elem_hbm, elem), (part_hbm, part), (flag_hbm, flag), (cot_hbm, cot), (feat_hbm, feat))
    ):
        copy = pltpu.make_async_copy(source, held, local_sems.at[n])
        copy.start()
        local.append(copy)

    pl.semaphore_wait(barrier, 3)

    sends = []

    def send(source, held, target):
        n = len(sends)
        copy = pltpu.make_async_remote_copy(
            src_ref=source, dst_ref=held, send_sem=send_sems.at[n], recv_sem=recv_sems.at[n],
            device_id=target, device_id_type=MESH,
        )
        copy.start()
        sends.append(copy)
        return copy

    pair_small = [
        send(pos_hbm, z_pos, pair_id), send(elem_hbm, z_elem, pair_id),
        send(part_hbm, z_part, pair_id), send(flag_hbm, z_flag, pair_id),
    ]
    prev_small = [
        send(pos_hbm, p_pos, next_id), send(elem_hbm, p_elem, next_id),
        send(part_hbm, p_part, next_id), send(flag_hbm, p_flag, next_id),
    ]
    next_small = [send(pos_hbm, n_pos, prev_id), send(elem_hbm, n_elem, prev_id)]
    pair_big = [send(cot_hbm, z_cot, pair_id)]
    next_big = [send(cot_hbm.at[0], n_cot, prev_id), send(feat_hbm.at[0], n_feat, prev_id)]
    prev_big = [send(cot_hbm, p_cot, next_id), send(feat_hbm, p_feat, next_id)]

    def rows_of(pos_ref, elem_ref):
        kinds = elem_ref[...]
        charge = jnp.zeros(kinds.shape, F32)
        for e in range(table_ref.shape[0]):
            charge = charge + jnp.where(kinds == e, table_ref[e], 0.0)
        charge = charge.astype(BF16).astype(F32)
        return [pos_ref[k].astype(F32) for k in range(3)] + [charge]

    def count(part_ref, flag_ref, cluster):
        hit = jnp.where(part_ref[...] == cluster, flag_ref[...].astype(F32), 0.0)
        return jnp.sum(hit, axis=1, keepdims=True)

    for copy in local[:4]:
        copy.wait()
    mine = rows_of(pos, elem)
    stack = jnp.concatenate(
        [mine[k][i : i + 1] for i in range(2) for k in range(4)] + [jnp.zeros((120, 128), F32)], axis=0
    )
    columns = jnp.transpose(stack)
    for i in range(2):
        for k in range(4):
            n = i * 4 + k
            wide[i, k] = jnp.broadcast_to(columns[:, n : n + 1], (128, 128))

    def geometry(tile, rows, factor):
        i, _, j = tile
        slot = SLOT[tile]
        y = [rows[k][j : j + 1] for k in range(3)]
        scaled = rows[3][j : j + 1] * (coupling_strength * factor)

        def chunk(c, carry):
            here = pl.ds(c * ROWS, ROWS)
            dx = wide[i, 0, here, :] - y[0]
            dy = wide[i, 1, here, :] - y[1]
            dz = wide[i, 2, here, :] - y[2]
            r2 = (dx * dx + dy * dy + dz * dz) + soften
            inverse = lax.rsqrt(r2)
            fall = jnp.exp((-screening * screening) * r2)
            ratio = scaled_erfc(screening * (r2 * inverse)) * inverse
            term = (wide[i, 3, here, :] * scaled) * fall
            kernels[slot, here, :] = (term * ratio).astype(BF16)
            slopes[slot, here, :] = -(term * (inverse * inverse)) * (2.0 * screening / math.sqrt(math.pi) + ratio)
            return carry

        lax.fori_loop(0, 128 // ROWS, chunk, 0, unroll=True)

    def padded(rows, j):
        return jnp.concatenate(
            [rows[k][j : j + 1] for k in range(3)] + [jnp.ones((1, 128), F32), jnp.zeros((4, 128), F32)], axis=0
        )

    mine8 = [padded(mine, i) for i in range(2)]
    mine8h = [m.astype(BF16) for m in mine8]

    def weight(tile, pair):
        w = slopes[SLOT[tile]] * pair
        high = w.astype(BF16)
        return high, (w - high.astype(F32)).astype(BF16)

    def to_mine(i, w, other8h):
        s = nt(other8h, w[0]) + nt(other8h, w[1])
        return mine8[i] * s[3:4] - s

    def to_other(i, w, other8):
        s = nn(mine8h[i], w[0]) + nn(mine8h[i], w[1])
        return other8 * s[3:4] - s

    counts = count(part, flag, device * 2 + 1)
    counts0 = count(part, flag, device * 2)
    own = (0, OWN, 1)
    geometry(own, mine, counts[0:1] + counts0[1:2])
    for copy in local[4:]:
        copy.wait()
    w = weight(own, nt(cot[0], feat[1]) + nt(feat[0], cot[1]))
    pos_total = [to_mine(0, w, mine8h[1]), to_other(0, w, mine8[1])]
    kernel = kernels[SLOT[own]]
    feat_total = [nn(kernel, cot[1]), tn(kernel, cot[0])]

    for copy in pair_small:
        copy.wait_recv()
    theirs = rows_of(z_pos, z_elem)
    upper = (device + 1) * 2
    low = [count(part, flag, upper + j) for j in range(2)]
    high = [count(z_part, z_flag, device * 2 + i) for i in range(2)]
    for i in range(2):
        for j in range(2):
            factor = jnp.where(gz == 0, low[j][i : i + 1], high[i][j : j + 1])
            geometry((i, PAIR, j), theirs, factor)
    theirs8 = [padded(theirs, j) for j in range(2)]
    theirs8h = [m.astype(BF16) for m in theirs8]

    for copy in next_small:
        copy.wait_recv()
    side = rows_of(n_pos, n_elem)
    side_counts = count(part, flag, (after * 2 + gz) * 2)
    for i in range(2):
        geometry((i, NEXT, 0), side, side_counts[i : i + 1])
    side8h = padded(side, 0).astype(BF16)

    for copy in prev_small:
        copy.wait_recv()
    back = rows_of(p_pos, p_elem)
    back_counts = count(p_part, p_flag, device * 2)
    for j in range(2):
        geometry((0, PREV, j), back, back_counts[j : j + 1])
    back8h = [padded(back, j).astype(BF16) for j in range(2)]

    for copy in pair_big:
        copy.wait_recv()
    give = [None, None]
    for i in range(2):
        for j in range(2):
            tile = (i, PAIR, j)
            w = weight(tile, nt(feat[i], z_cot[j]))
            pos_total[i] = pos_total[i] + to_mine(i, w, theirs8h[j])
            term = to_other(i, w, theirs8[j])
            give[j] = term if give[j] is None else give[j] + term
            feat_total[i] = feat_total[i] + nn(kernels[SLOT[tile]], z_cot[j])
    for j in range(2):
        z_give[j] = give[j]
    pos_back = send(z_give, z_take, pair_id)

    for copy in next_big:
        copy.wait_recv()
    for i in range(2):
        tile = (i, NEXT, 0)
        w = weight(tile, nt(cot[i], n_feat[...]) + nt(feat[i], n_cot[...]))
        pos_total[i] = pos_total[i] + to_mine(i, w, side8h)
        feat_total[i] = feat_total[i] + nn(kernels[SLOT[tile]], n_cot[...])
    out_feat[1] = feat_total[1]

    for copy in prev_big:
        copy.wait_recv()
    for j in range(2):
        tile = (0, PREV, j)
        w = weight(tile, nt(cot[0], p_feat[j]) + nt(feat[0], p_cot[j]))
        pos_total[0] = pos_total[0] + to_mine(0, w, back8h[j])
        feat_total[0] = feat_total[0] + nn(kernels[SLOT[tile]], p_cot[j])
    out_feat[0] = feat_total[0]

    pos_back.wait_recv()
    for k in range(3):
        out_pos[k] = jnp.concatenate(
            [pos_total[i][k : k + 1] + z_take[i, k : k + 1] for i in range(2)], axis=0
        )
    for copy in sends:
        copy.wait_send()


def per_device(gx_size, gy_size, features, cotangent, positions, element_types, charge_table, partners, tile_real_flags):
    anywhere = pl.BlockSpec(memory_space=pl.ANY)
    inside = pl.BlockSpec(memory_space=pltpu.VMEM)
    clusters, atoms, channels = features.shape
    listed = partners.shape[1]
    big = (clusters, atoms, channels)
    small_pos = pltpu.VMEM((3, clusters, atoms), BF16)
    small_int = pltpu.VMEM((clusters, atoms), jnp.int32)
    lists = pltpu.VMEM((clusters, listed), jnp.int32)
    count = 16
    grad_feat, grad_pos = pl.pallas_call(
        lambda *refs: body(gx_size, gy_size, *refs),
        out_shape=(
            jax.ShapeDtypeStruct(big, F32),
            jax.ShapeDtypeStruct((3, clusters, atoms), F32),
        ),
        in_specs=[anywhere] * 4 + [pl.BlockSpec(memory_space=pltpu.SMEM)] + [anywhere] * 2,
        out_specs=(inside, inside),
        scratch_shapes=[
            pltpu.VMEM(big, BF16), pltpu.VMEM(big, BF16), small_pos, small_int, lists, lists,
            pltpu.VMEM(big[1:], BF16), pltpu.VMEM(big[1:], BF16), small_pos, small_int,
            pltpu.VMEM(big, BF16), pltpu.VMEM(big, BF16), small_pos, small_int, lists, lists,
            pltpu.VMEM(big, BF16), small_pos, small_int, lists, lists,
            pltpu.VMEM((clusters, 8, atoms), F32), pltpu.VMEM((clusters, 8, atoms), F32),
            pltpu.VMEM((clusters, 4, atoms, atoms), F32),
            pltpu.VMEM((len(TILES), atoms, atoms), BF16),
            pltpu.VMEM((len(TILES), atoms, atoms), F32),
            pltpu.SemaphoreType.DMA((6,)),
            pltpu.SemaphoreType.DMA((count,)),
            pltpu.SemaphoreType.DMA((count,)),
        ],
        compiler_params=pltpu.CompilerParams(collective_id=0, has_side_effects=True),
    )(features, cotangent, jnp.transpose(positions, (1, 0, 2)), element_types, charge_table, partners, tile_real_flags)
    return grad_feat, jnp.transpose(grad_pos, (1, 0, 2))


def solution(mesh):
    def run(*args):
        return per_device(mesh.shape["gx"], mesh.shape["gy"], *args)

    return jax.shard_map(
        run,
        mesh=mesh,
        in_specs=(
            P(AXES, None, None),
            P(AXES, None, None),
            P(AXES, None, None),
            P(AXES, None),
            P(),
            P(AXES, None),
            P(AXES, None),
        ),
        out_specs=(P(AXES, None, None), P(AXES, None, None)),
        check_vma=False,
    )
```

```python
import math

import jax
import jax.numpy as jnp
from jax import lax
from jax.experimental import pallas as pl
from jax.experimental.pallas import tpu as pltpu
from jax.sharding import PartitionSpec as P

coupling_strength = 0.0625
screening = 0.3
soften = 1.0

AXES = ("gx", "gy", "gz")
MESH = pl.DeviceIdType.MESH
F32, BF16 = jnp.float32, jnp.bfloat16
ROWS = 32

SHIFT = 2.5
SCALED_ERFC = (
    1.0540318489074707, 0.8046519160270691, 0.4539143443107605, 0.171249657869339,
    0.028358077630400658, -0.008383735083043575, -0.004801364149898291, 0.0004147369763813913,
    0.0006639317725785077, -2.737039358180482e-05, -7.203718996606767e-05,
)

OWN, NEXT, PREV, PAIR = "own", "next", "prev", "pair"
TILES = (
    (0, PAIR, 0), (0, PAIR, 1), (0, NEXT, 0), (0, PREV, 0), (0, PREV, 1), (0, OWN, 1),
    (1, PAIR, 0), (1, PAIR, 1), (1, NEXT, 0),
)
SLOT = {tile: n for n, tile in enumerate(TILES)}


def scaled_erfc(x):
    u = 1.0 / (x + SHIFT)
    v = (2.0 * SHIFT) * u - 1.0
    total = jnp.full_like(v, SCALED_ERFC[-1])
    for coefficient in SCALED_ERFC[-2::-1]:
        total = total * v + coefficient
    return total * u


def nt(a, b):
    return lax.dot_general(a, b, (((1,), (1,)), ((), ())), preferred_element_type=F32)


def nn(a, b):
    return lax.dot_general(a, b, (((1,), (0,)), ((), ())), preferred_element_type=F32)


def tn(a, b):
    return lax.dot_general(a, b, (((0,), (0,)), ((), ())), preferred_element_type=F32)


def body(
    gx_size, gy_size,
    feat_hbm, cot_hbm, pos_hbm, elem_hbm, table_ref, part_hbm, flag_hbm,
    out_feat, out_pos,
    feat, cot, pos, elem, part, flag,
    n_feat, n_cot, n_pos, n_elem,
    p_feat, p_cot, p_pos, p_elem, p_part, p_flag,
    z_cot, z_pos, z_elem, z_part, z_flag,
    z_give, z_take,
    wide, kernels, slopes, totals,
    local_sems, send_sems, recv_sems, entered,
):
    gx, gy, gz = lax.axis_index("gx"), lax.axis_index("gy"), lax.axis_index("gz")
    lanes = gx_size * gy_size
    lateral = gx * gy_size + gy
    after = lax.rem(lateral + 1, lanes)
    before = lax.rem(lateral + lanes - 1, lanes)
    next_id = (after // gy_size, lax.rem(after, gy_size), gz)
    prev_id = (before // gy_size, lax.rem(before, gy_size), gz)
    pair_id = (gx, gy, 1 - gz)
    device = lateral * 2 + gz

    late = lax.rem(lateral, lanes // 2) == 0

    barrier = pltpu.get_barrier_semaphore()
    for target in (prev_id, pair_id):
        pl.semaphore_signal(barrier, inc=1, device_id=target, device_id_type=MESH)

    local = []
    for n, (source, held) in enumerate(
        ((pos_hbm, pos), (elem_hbm, elem), (part_hbm, part), (flag_hbm, flag), (cot_hbm, cot), (feat_hbm, feat))
    ):
        copy = pltpu.make_async_copy(source, held, local_sems.at[n])
        copy.start()
        local.append(copy)

    pl.semaphore_wait(barrier, 2)
    pl.semaphore_signal(entered, inc=1, device_id=next_id, device_id_type=MESH)

    sends = []

    def remote(source, held, target):
        n = len(sends)
        copy = pltpu.make_async_remote_copy(
            src_ref=source, dst_ref=held, send_sem=send_sems.at[n], recv_sem=recv_sems.at[n],
            device_id=target, device_id_type=MESH,
        )
        sends.append(copy)
        return copy

    prev_small = [
        remote(pos_hbm, p_pos, next_id), remote(elem_hbm, p_elem, next_id),
        remote(part_hbm, p_part, next_id), remote(flag_hbm, p_flag, next_id),
    ]
    pair_small = [
        remote(pos_hbm, z_pos, pair_id), remote(elem_hbm, z_elem, pair_id),
        remote(part_hbm, z_part, pair_id), remote(flag_hbm, z_flag, pair_id),
    ]
    prev_big = [remote(cot_hbm, p_cot, next_id), remote(feat_hbm, p_feat, next_id)]
    pair_big = [remote(cot_hbm, z_cot, pair_id)]
    next_small = [remote(pos_hbm, n_pos, prev_id), remote(elem_hbm, n_elem, prev_id)]
    next_big = [remote(cot_hbm.at[0], n_cot, prev_id), remote(feat_hbm.at[0], n_feat, prev_id)]
    pos_back = remote(z_give, z_take, pair_id)
    for copy in prev_small + pair_small + prev_big + pair_big:
        copy.start()

    def send_back():
        pl.semaphore_wait(entered, 1)
        for copy in next_small + next_big:
            copy.start()

    def rows_of(pos_ref, elem_ref):
        kinds = elem_ref[...]
        charge = jnp.zeros(kinds.shape, F32)
        for e in range(table_ref.shape[0]):
            charge = charge + jnp.where(kinds == e, table_ref[e], 0.0)
        charge = charge.astype(BF16).astype(F32)
        return [pos_ref[k].astype(F32) for k in range(3)] + [charge]

    def count(part_ref, flag_ref, cluster):
        hit = jnp.where(part_ref[...] == cluster, flag_ref[...].astype(F32), 0.0)
        return jnp.sum(hit, axis=1, keepdims=True)

    for copy in local[:4]:
        copy.wait()
    mine = rows_of(pos, elem)
    stack = jnp.concatenate(
        [mine[k][i : i + 1] for i in range(2) for k in range(4)] + [jnp.zeros((120, 128), F32)], axis=0
    )
    columns = jnp.transpose(stack)
    for i in range(2):
        for k in range(4):
            n = i * 4 + k
            wide[i, k] = jnp.broadcast_to(columns[:, n : n + 1], (128, 128))

    def geometry(tile, rows, factor):
        i, _, j = tile
        slot = SLOT[tile]
        y = [rows[k][j : j + 1] for k in range(3)]
        scaled = rows[3][j : j + 1] * (coupling_strength * factor)

        def chunk(c, carry):
            here = pl.ds(c * ROWS, ROWS)
            dx = wide[i, 0, here, :] - y[0]
            dy = wide[i, 1, here, :] - y[1]
            dz = wide[i, 2, here, :] - y[2]
            r2 = (dx * dx + dy * dy + dz * dz) + soften
            inverse = lax.rsqrt(r2)
            fall = jnp.exp((-screening * screening) * r2)
            ratio = scaled_erfc(screening * (r2 * inverse)) * inverse
            term = (wide[i, 3, here, :] * scaled) * fall
            kernels[slot, here, :] = (term * ratio).astype(BF16)
            slopes[slot, here, :] = -(term * (inverse * inverse)) * (2.0 * screening / math.sqrt(math.pi) + ratio)
            return carry

        lax.fori_loop(0, 128 // ROWS, chunk, 0, unroll=True)

    def padded(rows, j):
        return jnp.concatenate(
            [rows[k][j : j + 1] for k in range(3)] + [jnp.ones((1, 128), F32), jnp.zeros((4, 128), F32)], axis=0
        )

    mine8 = [padded(mine, i) for i in range(2)]
    mine8h = [m.astype(BF16) for m in mine8]

    def weight(tile, pair):
        w = slopes[SLOT[tile]] * pair
        high = w.astype(BF16)
        return high, (w - high.astype(F32)).astype(BF16)

    def to_mine(i, w, other8h):
        s = nt(other8h, w[0]) + nt(other8h, w[1])
        return mine8[i] * s[3:4] - s

    def to_other(i, w, other8):
        s = nn(mine8h[i], w[0]) + nn(mine8h[i], w[1])
        return other8 * s[3:4] - s

    counts = count(part, flag, device * 2 + 1)
    counts0 = count(part, flag, device * 2)
    own = (0, OWN, 1)
    geometry(own, mine, counts[0:1] + counts0[1:2])
    for copy in local[4:]:
        copy.wait()
    w = weight(own, nt(cot[0], feat[1]) + nt(feat[0], cot[1]))
    totals[0] = to_mine(0, w, mine8h[1])
    totals[1] = to_other(0, w, mine8[1])
    kernel = kernels[SLOT[own]]
    out_feat[0] = nn(kernel, cot[1])
    out_feat[1] = tn(kernel, cot[0])

    pl.when(jnp.logical_not(late))(send_back)

    for copy in pair_small:
        copy.wait_recv()
    theirs = rows_of(z_pos, z_elem)
    upper = (device + 1) * 2
    low = [count(part, flag, upper + j) for j in range(2)]
    high = [count(z_part, z_flag, device * 2 + i) for i in range(2)]
    for i in range(2):
        for j in range(2):
            factor = jnp.where(gz == 0, low[j][i : i + 1], high[i][j : j + 1])
            geometry((i, PAIR, j), theirs, factor)
    theirs8 = [padded(theirs, j) for j in range(2)]
    theirs8h = [m.astype(BF16) for m in theirs8]
    for copy in pair_big:
        copy.wait_recv()
    for j in range(2):
        give = []
        for i in range(2):
            tile = (i, PAIR, j)
            w = weight(tile, nt(feat[i], z_cot[j]))
            totals[i] += to_mine(i, w, theirs8h[j])
            give.append(to_other(i, w, theirs8[j]))
            out_feat[i] += nn(kernels[SLOT[tile]], z_cot[j])
        z_give[j] = give[0] + give[1]
    pos_back.start()

    for copy in next_small:
        copy.wait_recv()
    side = rows_of(n_pos, n_elem)
    side_counts = count(part, flag, (after * 2 + gz) * 2)
    for i in range(2):
        geometry((i, NEXT, 0), side, side_counts[i : i + 1])
    side8h = padded(side, 0).astype(BF16)
    for copy in next_big:
        copy.wait_recv()
    for i in range(2):
        tile = (i, NEXT, 0)
        w = weight(tile, nt(cot[i], n_feat[...]) + nt(feat[i], n_cot[...]))
        totals[i] += to_mine(i, w, side8h)
        out_feat[i] += nn(kernels[SLOT[tile]], n_cot[...])

    pl.when(late)(send_back)

    for copy in prev_small:
        copy.wait_recv()
    back = rows_of(p_pos, p_elem)
    back_counts = count(p_part, p_flag, device * 2)
    for j in range(2):
        geometry((0, PREV, j), back, back_counts[j : j + 1])
    back8h = [padded(back, j).astype(BF16) for j in range(2)]
    pos_back.wait_recv()
    for copy in prev_big:
        copy.wait_recv()
    pos_total = [totals[i] + z_take[i] for i in range(2)]
    for j in range(2):
        tile = (0, PREV, j)
        w = weight(tile, nt(cot[0], p_feat[j]) + nt(feat[0], p_cot[j]))
        pos_total[0] = pos_total[0] + to_mine(0, w, back8h[j])
    out_feat[0] += nn(kernels[SLOT[(0, PREV, 0)]], p_cot[0]) + nn(kernels[SLOT[(0, PREV, 1)]], p_cot[1])
    for k in range(3):
        out_pos[k] = jnp.concatenate([pos_total[i][k : k + 1] for i in range(2)], axis=0)
    for copy in sends:
        copy.wait_send()


def store(feat_ref, pos_ref, out_feat, out_pos, sems):
    copies = [
        pltpu.make_async_copy(feat_ref, out_feat, sems.at[0]),
        pltpu.make_async_copy(pos_ref, out_pos, sems.at[1]),
    ]
    for copy in copies:
        copy.start()
    for copy in copies:
        copy.wait()


def per_device(gx_size, gy_size, features, cotangent, positions, element_types, charge_table, partners, tile_real_flags):
    anywhere = pl.BlockSpec(memory_space=pl.ANY)
    inside = pl.BlockSpec(memory_space=pltpu.VMEM)
    clusters, atoms, channels = features.shape
    listed = partners.shape[1]
    big = (clusters, atoms, channels)
    small_pos = pltpu.VMEM((3, clusters, atoms), BF16)
    small_int = pltpu.VMEM((clusters, atoms), jnp.int32)
    lists = pltpu.VMEM((clusters, listed), jnp.int32)
    count = 16
    grad_feat, grad_pos = pl.pallas_call(
        lambda *refs: body(gx_size, gy_size, *refs),
        out_shape=(
            pltpu.VMEM(big, F32),
            pltpu.VMEM((3, clusters, atoms), F32),
        ),
        in_specs=[anywhere] * 4 + [pl.BlockSpec(memory_space=pltpu.SMEM)] + [anywhere] * 2,
        out_specs=(inside, inside),
        scratch_shapes=[
            pltpu.VMEM(big, BF16), pltpu.VMEM(big, BF16), small_pos, small_int, lists, lists,
            pltpu.VMEM(big[1:], BF16), pltpu.VMEM(big[1:], BF16), small_pos, small_int,
            pltpu.VMEM(big, BF16), pltpu.VMEM(big, BF16), small_pos, small_int, lists, lists,
            pltpu.VMEM(big, BF16), small_pos, small_int, lists, lists,
            pltpu.VMEM((clusters, 8, atoms), F32), pltpu.VMEM((clusters, 8, atoms), F32),
            pltpu.VMEM((clusters, 4, atoms, atoms), F32),
            pltpu.VMEM((len(TILES), atoms, atoms), BF16),
            pltpu.VMEM((len(TILES), atoms, atoms), F32),
            pltpu.VMEM((clusters, 8, atoms), F32),
            pltpu.SemaphoreType.DMA((6,)),
            pltpu.SemaphoreType.DMA((count,)),
            pltpu.SemaphoreType.DMA((count,)),
            pltpu.SemaphoreType.REGULAR,
        ],
        compiler_params=pltpu.CompilerParams(collective_id=0, has_side_effects=True),
    )(features, cotangent, jnp.transpose(positions, (1, 0, 2)), element_types, charge_table, partners, tile_real_flags)
    grad_feat, grad_pos = pl.pallas_call(
        store,
        out_shape=(
            jax.ShapeDtypeStruct(big, F32),
            jax.ShapeDtypeStruct((3, clusters, atoms), F32),
        ),
        in_specs=[inside, inside],
        out_specs=(anywhere, anywhere),
        scratch_shapes=[pltpu.SemaphoreType.DMA((2,))],
    )(*[pltpu.with_memory_space_constraint(x, pltpu.VMEM) for x in (grad_feat, grad_pos)])
    return grad_feat, jnp.transpose(grad_pos, (1, 0, 2))


def solution(mesh):
    def run(*args):
        return per_device(mesh.shape["gx"], mesh.shape["gy"], *args)

    return jax.shard_map(
        run,
        mesh=mesh,
        in_specs=(
            P(AXES, None, None),
            P(AXES, None, None),
            P(AXES, None, None),
            P(AXES, None),
            P(),
            P(AXES, None),
            P(AXES, None),
        ),
        out_specs=(P(AXES, None, None), P(AXES, None, None)),
        check_vma=False,
    )
```

```python
import math

import jax
import jax.numpy as jnp
from jax import lax
from jax.experimental import pallas as pl
from jax.experimental.pallas import tpu as pltpu
from jax.sharding import PartitionSpec as P

coupling_strength = 0.0625
screening = 0.3
soften = 1.0

AXES = ("gx", "gy", "gz")
MESH = pl.DeviceIdType.MESH
F32, BF16 = jnp.float32, jnp.bfloat16
ROWS = 32

SHIFT = 2.5
SCALED_ERFC = (
    1.0540318489074707, 0.8046519160270691, 0.4539143443107605, 0.171249657869339,
    0.028358077630400658, -0.008383735083043575, -0.004801364149898291, 0.0004147369763813913,
    0.0006639317725785077, -2.737039358180482e-05, -7.203718996606767e-05,
)

OWN, NEXT, PREV, PAIR = "own", "next", "prev", "pair"
TILES = (
    (0, PAIR, 0), (0, PAIR, 1), (0, NEXT, 0), (0, PREV, 0), (0, PREV, 1), (0, OWN, 1),
    (1, PAIR, 0), (1, PAIR, 1), (1, NEXT, 0),
)
SLOT = {tile: n for n, tile in enumerate(TILES)}


def scaled_erfc(x):
    u = 1.0 / (x + SHIFT)
    v = (2.0 * SHIFT) * u - 1.0
    total = jnp.full_like(v, SCALED_ERFC[-1])
    for coefficient in SCALED_ERFC[-2::-1]:
        total = total * v + coefficient
    return total * u


def nt(a, b):
    return lax.dot_general(a, b, (((1,), (1,)), ((), ())), preferred_element_type=F32)


def nn(a, b):
    return lax.dot_general(a, b, (((1,), (0,)), ((), ())), preferred_element_type=F32)


def tn(a, b):
    return lax.dot_general(a, b, (((0,), (0,)), ((), ())), preferred_element_type=F32)


def body(
    gx_size, gy_size,
    feat_hbm, cot_hbm, pos_hbm, elem_hbm, table_hbm, part_hbm, flag_hbm,
    out_feat, out_pos,
    feat, cot, pos, elem, part, flag,
    n_feat, n_cot, n_pos, n_elem,
    p_feat, p_cot, p_pos, p_elem, p_part, p_flag,
    z_cot, z_pos, z_elem, z_part, z_flag,
    z_give, z_take,
    wide, kernels, slopes, totals, table_ref,
    local_sems, send_sems, recv_sems, entered, told,
):
    gx, gy, gz = lax.axis_index("gx"), lax.axis_index("gy"), lax.axis_index("gz")
    lanes = gx_size * gy_size
    lateral = gx * gy_size + gy
    after = lax.rem(lateral + 1, lanes)
    before = lax.rem(lateral + lanes - 1, lanes)
    next_id = (after // gy_size, lax.rem(after, gy_size), gz)
    prev_id = (before // gy_size, lax.rem(before, gy_size), gz)
    pair_id = (gx, gy, 1 - gz)
    device = lateral * 2 + gz

    late = lax.rem(lateral, lanes // 2) == 0

    first = lax.rem(lateral + 1, lanes // 2) == 0
    teller = lax.rem(lateral + 2, lanes // 2) == 0

    barrier = pltpu.get_barrier_semaphore()
    pl.semaphore_signal(barrier, inc=1, device_id=prev_id, device_id_type=MESH)

    @pl.when(jnp.logical_not(first))
    def _():
        pl.semaphore_signal(barrier, inc=1, device_id=pair_id, device_id_type=MESH)

    local = []
    for n, (source, held) in enumerate(
        ((table_hbm, table_ref), (pos_hbm, pos), (elem_hbm, elem), (part_hbm, part), (flag_hbm, flag), (cot_hbm, cot), (feat_hbm, feat))
    ):
        copy = pltpu.make_async_copy(source, held, local_sems.at[n])
        copy.start()
        local.append(copy)

    pl.semaphore_wait(barrier, jnp.where(first, 1, 2))
    pl.semaphore_signal(entered, inc=1, device_id=next_id, device_id_type=MESH)

    sends = []

    def remote(source, held, target):
        n = len(sends)
        copy = pltpu.make_async_remote_copy(
            src_ref=source, dst_ref=held, send_sem=send_sems.at[n], recv_sem=recv_sems.at[n],
            device_id=target, device_id_type=MESH,
        )
        sends.append(copy)
        return copy

    prev_small = [
        remote(pos_hbm, p_pos, next_id), remote(elem_hbm, p_elem, next_id),
        remote(part_hbm, p_part, next_id), remote(flag_hbm, p_flag, next_id),
    ]
    pair_small = [
        remote(pos_hbm, z_pos, pair_id), remote(elem_hbm, z_elem, pair_id),
        remote(part_hbm, z_part, pair_id), remote(flag_hbm, z_flag, pair_id),
    ]
    prev_big = [remote(cot_hbm, p_cot, next_id), remote(feat_hbm, p_feat, next_id)]
    pair_big = [remote(cot_hbm, z_cot, pair_id)]
    next_small = [remote(pos_hbm, n_pos, prev_id), remote(elem_hbm, n_elem, prev_id)]
    next_big = [remote(cot_hbm.at[0], n_cot, prev_id), remote(feat_hbm.at[0], n_feat, prev_id)]
    pos_back = remote(z_give, z_take, pair_id)
    for copy in prev_small + prev_big:
        copy.start()

    @pl.when(teller)
    def _():
        pl.semaphore_signal(told, inc=1, device_id=pair_id, device_id_type=MESH)
        pl.semaphore_wait(told, 1)
        pl.semaphore_signal(told, inc=1, device_id=next_id, device_id_type=MESH)

    @pl.when(first)
    def _():
        pl.semaphore_wait(told, 1)

    for copy in pair_small + pair_big:
        copy.start()

    def send_back():
        pl.semaphore_wait(entered, 1)
        for copy in next_small + next_big:
            copy.start()

    def rows_of(pos_ref, elem_ref):
        kinds = elem_ref[...]
        charge = jnp.zeros(kinds.shape, F32)
        for e in range(table_ref.shape[0]):
            charge = charge + jnp.where(kinds == e, table_ref[e], 0.0)
        charge = charge.astype(BF16).astype(F32)
        return [pos_ref[k].astype(F32) for k in range(3)] + [charge]

    def count(part_ref, flag_ref, cluster):
        hit = jnp.where(part_ref[...] == cluster, flag_ref[...].astype(F32), 0.0)
        return jnp.sum(hit, axis=1, keepdims=True)

    for copy in local[:5]:
        copy.wait()
    mine = rows_of(pos, elem)
    stack = jnp.concatenate(
        [mine[k][i : i + 1] for i in range(2) for k in range(4)] + [jnp.zeros((120, 128), F32)], axis=0
    )
    columns = jnp.transpose(stack)
    for i in range(2):
        for k in range(4):
            n = i * 4 + k
            wide[i, k] = jnp.broadcast_to(columns[:, n : n + 1], (128, 128))

    def geometry(tile, rows, factor):
        i, _, j = tile
        slot = SLOT[tile]
        y = [rows[k][j : j + 1] for k in range(3)]
        scaled = rows[3][j : j + 1] * (coupling_strength * factor)

        def chunk(c, carry):
            here = pl.ds(c * ROWS, ROWS)
            dx = wide[i, 0, here, :] - y[0]
            dy = wide[i, 1, here, :] - y[1]
            dz = wide[i, 2, here, :] - y[2]
            r2 = (dx * dx + dy * dy + dz * dz) + soften
            inverse = lax.rsqrt(r2)
            fall = jnp.exp((-screening * screening) * r2)
            ratio = scaled_erfc(screening * (r2 * inverse)) * inverse
            term = (wide[i, 3, here, :] * scaled) * fall
            kernels[slot, here, :] = (term * ratio).astype(BF16)
            slopes[slot, here, :] = -(term * (inverse * inverse)) * (2.0 * screening / math.sqrt(math.pi) + ratio)
            return carry

        lax.fori_loop(0, 128 // ROWS, chunk, 0, unroll=True)

    def padded(rows, j):
        return jnp.concatenate(
            [rows[k][j : j + 1] for k in range(3)] + [jnp.ones((1, 128), F32), jnp.zeros((4, 128), F32)], axis=0
        )

    mine8 = [padded(mine, i) for i in range(2)]
    mine8h = [m.astype(BF16) for m in mine8]

    def weight(tile, pair):
        w = slopes[SLOT[tile]] * pair
        high = w.astype(BF16)
        return high, (w - high.astype(F32)).astype(BF16)

    def to_mine(i, w, other8h):
        s = nt(other8h, w[0]) + nt(other8h, w[1])
        return mine8[i] * s[3:4] - s

    def to_other(i, w, other8):
        s = nn(mine8h[i], w[0]) + nn(mine8h[i], w[1])
        return other8 * s[3:4] - s

    counts = count(part, flag, device * 2 + 1)
    counts0 = count(part, flag, device * 2)
    own = (0, OWN, 1)
    geometry(own, mine, counts[0:1] + counts0[1:2])
    for copy in local[5:]:
        copy.wait()
    w = weight(own, nt(cot[0], feat[1]) + nt(feat[0], cot[1]))
    totals[0] = to_mine(0, w, mine8h[1])
    totals[1] = to_other(0, w, mine8[1])
    kernel = kernels[SLOT[own]]
    out_feat[0] = nn(kernel, cot[1])
    out_feat[1] = tn(kernel, cot[0])

    pl.when(jnp.logical_not(late))(send_back)

    for copy in pair_small:
        copy.wait_recv()
    theirs = rows_of(z_pos, z_elem)
    upper = (device + 1) * 2
    low = [count(part, flag, upper + j) for j in range(2)]
    high = [count(z_part, z_flag, device * 2 + i) for i in range(2)]
    for i in range(2):
        for j in range(2):
            factor = jnp.where(gz == 0, low[j][i : i + 1], high[i][j : j + 1])
            geometry((i, PAIR, j), theirs, factor)
    theirs8 = [padded(theirs, j) for j in range(2)]
    theirs8h = [m.astype(BF16) for m in theirs8]
    for copy in pair_big:
        copy.wait_recv()
    for j in range(2):
        give = []
        for i in range(2):
            tile = (i, PAIR, j)
            w = weight(tile, nt(feat[i], z_cot[j]))
            totals[i] += to_mine(i, w, theirs8h[j])
            give.append(to_other(i, w, theirs8[j]))
            out_feat[i] += nn(kernels[SLOT[tile]], z_cot[j])
        z_give[j] = give[0] + give[1]
    pos_back.start()

    for copy in next_small:
        copy.wait_recv()
    side = rows_of(n_pos, n_elem)
    side_counts = count(part, flag, (after * 2 + gz) * 2)
    for i in range(2):
        geometry((i, NEXT, 0), side, side_counts[i : i + 1])
    side8h = padded(side, 0).astype(BF16)
    for copy in next_big:
        copy.wait_recv()
    for i in range(2):
        tile = (i, NEXT, 0)
        w = weight(tile, nt(cot[i], n_feat[...]) + nt(feat[i], n_cot[...]))
        totals[i] += to_mine(i, w, side8h)
        out_feat[i] += nn(kernels[SLOT[tile]], n_cot[...])

    pl.when(late)(send_back)

    for copy in prev_small:
        copy.wait_recv()
    back = rows_of(p_pos, p_elem)
    back_counts = count(p_part, p_flag, device * 2)
    for j in range(2):
        geometry((0, PREV, j), back, back_counts[j : j + 1])
    back8h = [padded(back, j).astype(BF16) for j in range(2)]
    pos_back.wait_recv()
    for copy in prev_big:
        copy.wait_recv()
    pos_total = [totals[i] + z_take[i] for i in range(2)]
    for j in range(2):
        tile = (0, PREV, j)
        w = weight(tile, nt(cot[0], p_feat[j]) + nt(feat[0], p_cot[j]))
        pos_total[0] = pos_total[0] + to_mine(0, w, back8h[j])
    out_feat[0] += nn(kernels[SLOT[(0, PREV, 0)]], p_cot[0]) + nn(kernels[SLOT[(0, PREV, 1)]], p_cot[1])
    for k in range(3):
        out_pos[k] = jnp.concatenate([pos_total[i][k : k + 1] for i in range(2)], axis=0)
    for copy in sends:
        copy.wait_send()


def store(feat_ref, pos_ref, out_feat, out_pos, sems):
    copies = [
        pltpu.make_async_copy(feat_ref, out_feat, sems.at[0]),
        pltpu.make_async_copy(pos_ref, out_pos, sems.at[1]),
    ]
    for copy in copies:
        copy.start()
    for copy in copies:
        copy.wait()


def per_device(gx_size, gy_size, features, cotangent, positions, element_types, charge_table, partners, tile_real_flags):
    anywhere = pl.BlockSpec(memory_space=pl.ANY)
    inside = pl.BlockSpec(memory_space=pltpu.VMEM)
    clusters, atoms, channels = features.shape
    listed = partners.shape[1]
    big = (clusters, atoms, channels)
    small_pos = pltpu.VMEM((3, clusters, atoms), BF16)
    small_int = pltpu.VMEM((clusters, atoms), jnp.int32)
    lists = pltpu.VMEM((clusters, listed), jnp.int32)
    count = 16
    grad_feat, grad_pos = pl.pallas_call(
        lambda *refs: body(gx_size, gy_size, *refs),
        out_shape=(
            pltpu.VMEM(big, F32),
            pltpu.VMEM((3, clusters, atoms), F32),
        ),
        in_specs=[anywhere] * 7,
        out_specs=(inside, inside),
        scratch_shapes=[
            pltpu.VMEM(big, BF16), pltpu.VMEM(big, BF16), small_pos, small_int, lists, lists,
            pltpu.VMEM(big[1:], BF16), pltpu.VMEM(big[1:], BF16), small_pos, small_int,
            pltpu.VMEM(big, BF16), pltpu.VMEM(big, BF16), small_pos, small_int, lists, lists,
            pltpu.VMEM(big, BF16), small_pos, small_int, lists, lists,
            pltpu.VMEM((clusters, 8, atoms), F32), pltpu.VMEM((clusters, 8, atoms), F32),
            pltpu.VMEM((clusters, 4, atoms, atoms), F32),
            pltpu.VMEM((len(TILES), atoms, atoms), BF16),
            pltpu.VMEM((len(TILES), atoms, atoms), F32),
            pltpu.VMEM((clusters, 8, atoms), F32),
            pltpu.SMEM(charge_table.shape, F32),
            pltpu.SemaphoreType.DMA((7,)),
            pltpu.SemaphoreType.DMA((count,)),
            pltpu.SemaphoreType.DMA((count,)),
            pltpu.SemaphoreType.REGULAR,
            pltpu.SemaphoreType.REGULAR,
        ],
        compiler_params=pltpu.CompilerParams(collective_id=0, has_side_effects=True),
    )(features, cotangent, jnp.transpose(positions, (1, 0, 2)), element_types, charge_table, partners, tile_real_flags)
    grad_feat, grad_pos = pl.pallas_call(
        store,
        out_shape=(
            jax.ShapeDtypeStruct(big, F32),
            jax.ShapeDtypeStruct((3, clusters, atoms), F32),
        ),
        in_specs=[inside, inside],
        out_specs=(anywhere, anywhere),
        scratch_shapes=[pltpu.SemaphoreType.DMA((2,))],
    )(*[pltpu.with_memory_space_constraint(x, pltpu.VMEM) for x in (grad_feat, grad_pos)])
    return grad_feat, jnp.transpose(grad_pos, (1, 0, 2))


def solution(mesh):
    def run(*args):
        return per_device(mesh.shape["gx"], mesh.shape["gy"], *args)

    return jax.shard_map(
        run,
        mesh=mesh,
        in_specs=(
            P(AXES, None, None),
            P(AXES, None, None),
            P(AXES, None, None),
            P(AXES, None),
            P(),
            P(AXES, None),
            P(AXES, None),
        ),
        out_specs=(P(AXES, None, None), P(AXES, None, None)),
        check_vma=False,
    )
```

```python
import math

import jax
import jax.numpy as jnp
from jax import lax
from jax.experimental import pallas as pl
from jax.experimental.pallas import tpu as pltpu
from jax.sharding import PartitionSpec as P

coupling_strength = 0.0625
screening = 0.3
soften = 1.0

AXES = ("gx", "gy", "gz")
MESH = pl.DeviceIdType.MESH
F32, BF16 = jnp.float32, jnp.bfloat16
ROWS = 32
PIECES = 2

SHIFT = 2.5
SCALED_ERFC = (
    1.0540318489074707, 0.8046519160270691, 0.4539143443107605, 0.171249657869339,
    0.028358077630400658, -0.008383735083043575, -0.004801364149898291, 0.0004147369763813913,
    0.0006639317725785077, -2.737039358180482e-05, -7.203718996606767e-05,
)

OWN, NEXT, PREV, PAIR = "own", "next", "prev", "pair"
TILES = (
    (0, PAIR, 0), (0, PAIR, 1), (0, NEXT, 0), (0, PREV, 0), (0, PREV, 1), (0, OWN, 1),
    (1, PAIR, 0), (1, PAIR, 1), (1, NEXT, 0),
)
SLOT = {tile: n for n, tile in enumerate(TILES)}


def scaled_erfc(x):
    u = 1.0 / (x + SHIFT)
    v = (2.0 * SHIFT) * u - 1.0
    total = jnp.full_like(v, SCALED_ERFC[-1])
    for coefficient in SCALED_ERFC[-2::-1]:
        total = total * v + coefficient
    return total * u


def nt(a, b):
    return lax.dot_general(a, b, (((1,), (1,)), ((), ())), preferred_element_type=F32)


def nn(a, b):
    return lax.dot_general(a, b, (((1,), (0,)), ((), ())), preferred_element_type=F32)


def tn(a, b):
    return lax.dot_general(a, b, (((0,), (0,)), ((), ())), preferred_element_type=F32)


def body(
    gx_size, gy_size,
    feat_hbm, cot_hbm, pos_hbm, elem_hbm, table_hbm, part_hbm, flag_hbm,
    out_feat, out_pos,
    feat, cot, pos, elem, part, flag,
    n_feat, n_cot, n_pos, n_elem,
    p_feat, p_cot, p_pos, p_elem, p_part, p_flag,
    z_cot, z_pos, z_elem, z_part, z_flag,
    z_give, z_take, hold,
    wide, kernels, slopes, totals, table_ref,
    local_sems, send_sems, recv_sems, entered, told,
):
    gx, gy, gz = lax.axis_index("gx"), lax.axis_index("gy"), lax.axis_index("gz")
    lanes = gx_size * gy_size
    lateral = gx * gy_size + gy
    after = lax.rem(lateral + 1, lanes)
    before = lax.rem(lateral + lanes - 1, lanes)
    next_id = (after // gy_size, lax.rem(after, gy_size), gz)
    prev_id = (before // gy_size, lax.rem(before, gy_size), gz)
    pair_id = (gx, gy, 1 - gz)
    device = lateral * 2 + gz

    late = lax.rem(lateral, lanes // 2) == 0

    first = lax.rem(lateral + 1, lanes // 2) == 0
    teller = lax.rem(lateral + 2, lanes // 2) == 0

    middle = lax.rem(lateral, lanes // 2) == lanes // 2 - gy_size + 1
    start = lateral - lax.rem(lateral, lanes // 2)
    across = lax.rem(start + lanes // 2, lanes)

    def device_at(where):
        return (where // gy_size, lax.rem(where, gy_size), gz)

    barrier = pltpu.get_barrier_semaphore()
    pl.semaphore_signal(barrier, inc=1, device_id=prev_id, device_id_type=MESH)

    @pl.when(jnp.logical_not(first))
    def _():
        pl.semaphore_signal(barrier, inc=1, device_id=pair_id, device_id_type=MESH)

    local = []
    for n, (source, held) in enumerate(
        ((table_hbm, table_ref), (pos_hbm, pos), (elem_hbm, elem), (part_hbm, part), (flag_hbm, flag), (cot_hbm, cot), (feat_hbm, feat))
    ):
        copy = pltpu.make_async_copy(source, held, local_sems.at[n])
        copy.start()
        local.append(copy)

    @pl.when(middle)
    def _():
        pl.semaphore_signal(barrier, inc=1, device_id=device_at(start + lanes // 2 - 1), device_id_type=MESH)

    @pl.when(late)
    def _():
        pl.semaphore_signal(barrier, inc=1, device_id=device_at(across + lanes // 2 - gy_size + 1), device_id_type=MESH)

    pl.semaphore_wait(barrier, jnp.where(middle, 3, 2))
    pl.semaphore_signal(entered, inc=1, device_id=next_id, device_id_type=MESH)

    sends = []

    def remote(source, held, target, arrival=None):
        n = len(sends)
        copy = pltpu.make_async_remote_copy(
            src_ref=source, dst_ref=held, send_sem=send_sems.at[n],
            recv_sem=recv_sems.at[n if arrival is None else arrival],
            device_id=target, device_id_type=MESH,
        )
        sends.append(copy)
        return copy

    prev_small = [
        remote(pos_hbm, p_pos, next_id), remote(elem_hbm, p_elem, next_id),
        remote(part_hbm, p_part, next_id), remote(flag_hbm, p_flag, next_id),
    ]
    pair_small = [
        remote(pos_hbm, z_pos, pair_id), remote(elem_hbm, z_elem, pair_id),
        remote(part_hbm, z_part, pair_id), remote(flag_hbm, z_flag, pair_id),
    ]
    prev_big = [remote(cot_hbm, p_cot, next_id), remote(feat_hbm.at[0], p_feat.at[0], next_id)]
    pair_big = [remote(cot_hbm, z_cot, pair_id)]
    next_small = [remote(pos_hbm, n_pos, prev_id), remote(elem_hbm, n_elem, prev_id)]
    next_big = [remote(cot_hbm.at[0], n_cot, prev_id), remote(feat_hbm.at[0], n_feat, prev_id)]
    pos_back = remote(z_give, z_take, pair_id)
    always = list(sends)
    pieces = [pl.ds(at, feat.shape[1] // PIECES) for at in range(0, feat.shape[1], feat.shape[1] // PIECES)]
    relay = device_at(start + lanes // 2 - gy_size + 1)
    target = device_at(across)
    base = len(sends)
    direct = [remote(feat_hbm.at[1, rows], p_feat.at[1, rows], next_id) for rows in pieces]
    relayed = [remote(feat_hbm.at[1, rows], hold.at[rows], relay) for rows in pieces]
    handed = [
        remote(hold.at[rows], p_feat.at[1, rows], target, base + n) for n, rows in enumerate(pieces)
    ]

    @pl.when(first)
    def _():
        for copy in relayed:
            copy.start()

    for copy in prev_small + prev_big:
        copy.start()

    @pl.when(jnp.logical_not(first))
    def _():
        for copy in direct:
            copy.start()

    @pl.when(teller)
    def _():
        pl.semaphore_signal(told, inc=1, device_id=pair_id, device_id_type=MESH)
        pl.semaphore_wait(told, 1)
        pl.semaphore_signal(told, inc=1, device_id=next_id, device_id_type=MESH)

    @pl.when(first)
    def _():
        pl.semaphore_wait(told, 1)

    for copy in pair_small + pair_big:
        copy.start()

    @pl.when(middle)
    def _():
        for n, copy in enumerate(relayed):
            copy.wait_recv()
            handed[n].start()

    def send_back():
        pl.semaphore_wait(entered, 1)
        for copy in next_small + next_big:
            copy.start()

    def rows_of(pos_ref, elem_ref):
        kinds = elem_ref[...]
        charge = jnp.zeros(kinds.shape, F32)
        for e in range(table_ref.shape[0]):
            charge = charge + jnp.where(kinds == e, table_ref[e], 0.0)
        charge = charge.astype(BF16).astype(F32)
        return [pos_ref[k].astype(F32) for k in range(3)] + [charge]

    def count(part_ref, flag_ref, cluster):
        hit = jnp.where(part_ref[...] == cluster, flag_ref[...].astype(F32), 0.0)
        return jnp.sum(hit, axis=1, keepdims=True)

    for copy in local[:5]:
        copy.wait()
    mine = rows_of(pos, elem)
    stack = jnp.concatenate(
        [mine[k][i : i + 1] for i in range(2) for k in range(4)] + [jnp.zeros((120, 128), F32)], axis=0
    )
    columns = jnp.transpose(stack)
    for i in range(2):
        for k in range(4):
            n = i * 4 + k
            wide[i, k] = jnp.broadcast_to(columns[:, n : n + 1], (128, 128))

    def geometry(tile, rows, factor):
        i, _, j = tile
        slot = SLOT[tile]
        y = [rows[k][j : j + 1] for k in range(3)]
        scaled = rows[3][j : j + 1] * (coupling_strength * factor)

        def chunk(c, carry):
            here = pl.ds(c * ROWS, ROWS)
            dx = wide[i, 0, here, :] - y[0]
            dy = wide[i, 1, here, :] - y[1]
            dz = wide[i, 2, here, :] - y[2]
            r2 = (dx * dx + dy * dy + dz * dz) + soften
            inverse = lax.rsqrt(r2)
            fall = jnp.exp((-screening * screening) * r2)
            ratio = scaled_erfc(screening * (r2 * inverse)) * inverse
            term = (wide[i, 3, here, :] * scaled) * fall
            kernels[slot, here, :] = (term * ratio).astype(BF16)
            slopes[slot, here, :] = -(term * (inverse * inverse)) * (2.0 * screening / math.sqrt(math.pi) + ratio)
            return carry

        lax.fori_loop(0, 128 // ROWS, chunk, 0, unroll=True)

    def padded(rows, j):
        return jnp.concatenate(
            [rows[k][j : j + 1] for k in range(3)] + [jnp.ones((1, 128), F32), jnp.zeros((4, 128), F32)], axis=0
        )

    mine8 = [padded(mine, i) for i in range(2)]
    mine8h = [m.astype(BF16) for m in mine8]

    def weight(tile, pair):
        w = slopes[SLOT[tile]] * pair
        high = w.astype(BF16)
        return high, (w - high.astype(F32)).astype(BF16)

    def to_mine(i, w, other8h):
        s = nt(other8h, w[0]) + nt(other8h, w[1])
        return mine8[i] * s[3:4] - s

    def to_other(i, w, other8):
        s = nn(mine8h[i], w[0]) + nn(mine8h[i], w[1])
        return other8 * s[3:4] - s

    counts = count(part, flag, device * 2 + 1)
    counts0 = count(part, flag, device * 2)
    own = (0, OWN, 1)
    geometry(own, mine, counts[0:1] + counts0[1:2])
    for copy in local[5:]:
        copy.wait()
    w = weight(own, nt(cot[0], feat[1]) + nt(feat[0], cot[1]))
    totals[0] = to_mine(0, w, mine8h[1])
    totals[1] = to_other(0, w, mine8[1])
    kernel = kernels[SLOT[own]]
    out_feat[0] = nn(kernel, cot[1])
    out_feat[1] = tn(kernel, cot[0])

    pl.when(jnp.logical_not(late))(send_back)

    for copy in pair_small:
        copy.wait_recv()
    theirs = rows_of(z_pos, z_elem)
    upper = (device + 1) * 2
    low = [count(part, flag, upper + j) for j in range(2)]
    high = [count(z_part, z_flag, device * 2 + i) for i in range(2)]
    for i in range(2):
        for j in range(2):
            factor = jnp.where(gz == 0, low[j][i : i + 1], high[i][j : j + 1])
            geometry((i, PAIR, j), theirs, factor)
    theirs8 = [padded(theirs, j) for j in range(2)]
    theirs8h = [m.astype(BF16) for m in theirs8]
    for copy in pair_big:
        copy.wait_recv()
    for j in range(2):
        give = []
        for i in range(2):
            tile = (i, PAIR, j)
            w = weight(tile, nt(feat[i], z_cot[j]))
            totals[i] += to_mine(i, w, theirs8h[j])
            give.append(to_other(i, w, theirs8[j]))
            out_feat[i] += nn(kernels[SLOT[tile]], z_cot[j])
        z_give[j] = give[0] + give[1]
    pos_back.start()

    for copy in next_small:
        copy.wait_recv()
    side = rows_of(n_pos, n_elem)
    side_counts = count(part, flag, (after * 2 + gz) * 2)
    for i in range(2):
        geometry((i, NEXT, 0), side, side_counts[i : i + 1])
    side8h = padded(side, 0).astype(BF16)
    for copy in next_big:
        copy.wait_recv()
    for i in range(2):
        tile = (i, NEXT, 0)
        w = weight(tile, nt(cot[i], n_feat[...]) + nt(feat[i], n_cot[...]))
        totals[i] += to_mine(i, w, side8h)
        out_feat[i] += nn(kernels[SLOT[tile]], n_cot[...])

    pl.when(late)(send_back)

    for copy in prev_small:
        copy.wait_recv()
    back = rows_of(p_pos, p_elem)
    back_counts = count(p_part, p_flag, device * 2)
    for j in range(2):
        geometry((0, PREV, j), back, back_counts[j : j + 1])
    back8h = [padded(back, j).astype(BF16) for j in range(2)]
    pos_back.wait_recv()
    for copy in prev_big + direct:
        copy.wait_recv()
    pos_total = [totals[i] + z_take[i] for i in range(2)]
    for j in range(2):
        tile = (0, PREV, j)
        w = weight(tile, nt(cot[0], p_feat[j]) + nt(feat[0], p_cot[j]))
        pos_total[0] = pos_total[0] + to_mine(0, w, back8h[j])
    out_feat[0] += nn(kernels[SLOT[(0, PREV, 0)]], p_cot[0]) + nn(kernels[SLOT[(0, PREV, 1)]], p_cot[1])
    for k in range(3):
        out_pos[k] = jnp.concatenate([pos_total[i][k : k + 1] for i in range(2)], axis=0)
    for copy in always:
        copy.wait_send()

    @pl.when(jnp.logical_not(first))
    def _():
        for copy in direct:
            copy.wait_send()

    @pl.when(first)
    def _():
        for copy in relayed:
            copy.wait_send()

    @pl.when(middle)
    def _():
        for copy in handed:
            copy.wait_send()


def store(feat_ref, pos_ref, out_feat, out_pos, sems):
    copies = [
        pltpu.make_async_copy(feat_ref, out_feat, sems.at[0]),
        pltpu.make_async_copy(pos_ref, out_pos, sems.at[1]),
    ]
    for copy in copies:
        copy.start()
    for copy in copies:
        copy.wait()


def per_device(gx_size, gy_size, features, cotangent, positions, element_types, charge_table, partners, tile_real_flags):
    anywhere = pl.BlockSpec(memory_space=pl.ANY)
    inside = pl.BlockSpec(memory_space=pltpu.VMEM)
    clusters, atoms, channels = features.shape
    listed = partners.shape[1]
    big = (clusters, atoms, channels)
    small_pos = pltpu.VMEM((3, clusters, atoms), BF16)
    small_int = pltpu.VMEM((clusters, atoms), jnp.int32)
    lists = pltpu.VMEM((clusters, listed), jnp.int32)
    count = 16 + 3 * PIECES
    grad_feat, grad_pos = pl.pallas_call(
        lambda *refs: body(gx_size, gy_size, *refs),
        out_shape=(
            pltpu.VMEM(big, F32),
            pltpu.VMEM((3, clusters, atoms), F32),
        ),
        in_specs=[anywhere] * 7,
        out_specs=(inside, inside),
        scratch_shapes=[
            pltpu.VMEM(big, BF16), pltpu.VMEM(big, BF16), small_pos, small_int, lists, lists,
            pltpu.VMEM(big[1:], BF16), pltpu.VMEM(big[1:], BF16), small_pos, small_int,
            pltpu.VMEM(big, BF16), pltpu.VMEM(big, BF16), small_pos, small_int, lists, lists,
            pltpu.VMEM(big, BF16), small_pos, small_int, lists, lists,
            pltpu.VMEM((clusters, 8, atoms), F32), pltpu.VMEM((clusters, 8, atoms), F32),
            pltpu.VMEM(big[1:], BF16),
            pltpu.VMEM((clusters, 4, atoms, atoms), F32),
            pltpu.VMEM((len(TILES), atoms, atoms), BF16),
            pltpu.VMEM((len(TILES), atoms, atoms), F32),
            pltpu.VMEM((clusters, 8, atoms), F32),
            pltpu.SMEM(charge_table.shape, F32),
            pltpu.SemaphoreType.DMA((7,)),
            pltpu.SemaphoreType.DMA((count,)),
            pltpu.SemaphoreType.DMA((count,)),
            pltpu.SemaphoreType.REGULAR,
            pltpu.SemaphoreType.REGULAR,
        ],
        compiler_params=pltpu.CompilerParams(collective_id=0, has_side_effects=True),
    )(features, cotangent, jnp.transpose(positions, (1, 0, 2)), element_types, charge_table, partners, tile_real_flags)
    grad_feat, grad_pos = pl.pallas_call(
        store,
        out_shape=(
            jax.ShapeDtypeStruct(big, F32),
            jax.ShapeDtypeStruct((3, clusters, atoms), F32),
        ),
        in_specs=[inside, inside],
        out_specs=(anywhere, anywhere),
        scratch_shapes=[pltpu.SemaphoreType.DMA((2,))],
    )(*[pltpu.with_memory_space_constraint(x, pltpu.VMEM) for x in (grad_feat, grad_pos)])
    return grad_feat, jnp.transpose(grad_pos, (1, 0, 2))


def solution(mesh):
    def run(*args):
        return per_device(mesh.shape["gx"], mesh.shape["gy"], *args)

    return jax.shard_map(
        run,
        mesh=mesh,
        in_specs=(
            P(AXES, None, None),
            P(AXES, None, None),
            P(AXES, None, None),
            P(AXES, None),
            P(),
            P(AXES, None),
            P(AXES, None),
        ),
        out_specs=(P(AXES, None, None), P(AXES, None, None)),
        check_vma=False,
    )
```
